32 devices in a mesh: segment: 4 (over z), dp: 8 (over y, x, core).
Axes of the slice: x: 2, y: 2, z: 4, core: 2. Of those that a mesh axis runs over, the one named last changes fastest.
Arguments:
- images: bfloat16 [4, 16, 64, 256], P(None, 'dp'), may hold values from -6 to 6
- cotangent: bfloat16 [4, 16, 64, 256], P(None, 'dp'), may hold values from -0.059814453 to 0.059814453
- section_cells: int32 [4], replicated, may hold values from 1 to 8, as said below
- point_weight: bfloat16 [32, 256, 256], P('segment'), may hold values from -0.09375 to 0.09375
- tap_weight: float32 [32, 3, 256], P('segment'), may hold values from -3 to 3
Outputs:
- grad_point: float32 [32, 256, 256], P('segment', 'dp')
- grad_taps: float32 [32, 3, 256], P('segment')
The draws below stay inside these ranges and needn't reach their ends.
Inputs may be any that keep to these rules, and one draw needn't show every extreme that they name: `section_cells`: every section has at least one live slot, and in every draw some section has all 8 slots live.
All inputs are finite; a program needn't handle non-finite values.
Results may differ from the reference program's by a relative error of at most 0.015.
The reference program's roundings to bfloat16 on the way count: a program that leaves them out, or rounds other values in their place, can miss the bound.
Values may be sent and summed in bfloat16 or wider, within the bound.
No kernel may reach another device: no remote copies, remote signals or barrier semaphores. Data moves between devices by JAX's collectives and lax.ppermute only.
A program may use at most 64 MiB of HBM per device.

```python
import jax
import jax.numpy as jnp
from jax import lax

C = 256
W = 64
MICRO = 4
CELLS_DEV = 8
CELLS = 32
ROWS = 16
N_SEGMENT = 4


def draw_section_cells(key, part):
    first_key = jax.random.fold_in(key, 11)
    second_key = jax.random.fold_in(key, 12)
    drawn = jax.random.randint(first_key, (N_SEGMENT,), 1, CELLS_DEV + 1)
    fullest = jax.random.randint(second_key, (), 0, N_SEGMENT)
    return jnp.where(jnp.arange(N_SEGMENT) == fullest, CELLS_DEV, drawn).astype(jnp.int32)


def with_spikes(array, rng, source, target, shards_of, factor):
    owner, partner = [(jnp.arange(array.shape[axis_at]) // (array.shape[axis_at] // shards_of)).reshape([-1 if axis == axis_at else 1 for axis in range(array.ndim)]) for axis_at in (source, target)]
    chosen = jax.random.permutation(rng, shards_of)[partner]
    strong = (owner == chosen) | (owner == (partner + shards_of // 2) % shards_of)
    return jnp.where(strong, factor * array, array)


def shard_levels(stream_key, shape, shards, least, high):
    factor_of = 1.0
    for dim, blocks in shards:
        steps = jax.random.uniform(jax.random.fold_in(jax.random.fold_in(stream_key, 6), dim), (blocks,), jnp.float32, least / len(shards), high / len(shards))
        factor_of = factor_of * jnp.repeat(jnp.exp(steps), shape[dim] // blocks).reshape((-1,) + (1,) * (len(shape) - 1 - dim))
    return factor_of


def scatter_about(stream_key, dims, scale, bound, cuts=(), dtype=jnp.bfloat16):
    loudness = shard_levels(stream_key, dims, cuts, -0.22, 0.18) if cuts else 1.0
    entries = jax.random.normal(stream_key, dims, jnp.float32) * scale * loudness
    return jnp.minimum(jnp.maximum(entries, -bound), bound).astype(dtype)


def gaussian_with(key, extent, deviation, limit, split, heavy, held_as=jnp.bfloat16):
    values = deviation * jax.random.normal(key, extent, jnp.float32)
    if split:
        values = values * shard_levels(key, extent, split, -0.22, 0.18)
    return jnp.clip(with_spikes(values, jax.random.fold_in(key, 3), *heavy), -limit, limit).astype(held_as)


def setup_inputs(seed: int = 0) -> dict:
    arg_keys = jax.random.split(jax.random.key(seed), 6)
    return {
        "images": gaussian_with(arg_keys[0], (MICRO, ROWS, W, C), 1.0, 6.0, ((1, 8),), (1, 3, 8, 2.0)),
        "cotangent": scatter_about(arg_keys[1], (MICRO, ROWS, W, C), 0.01, 0.059814453, ((1, 8),)),
        "section_cells": draw_section_cells(jax.random.fold_in(arg_keys[5], 71), 0),
        "point_weight": scatter_about(arg_keys[3], (CELLS, C, C), (CELLS * C // 2) ** -0.5, 0.09375, ((0, 4),)),
        "tap_weight": scatter_about(arg_keys[4], (CELLS, 3, C), 0.5, 3.0, ((0, 4),), jnp.float32),
    }


def shifted(values, dilation):
    padding = jnp.zeros_like(values[:, :dilation, :])
    before = jnp.concatenate([padding, values[:, :-dilation, :]], axis=1)
    beyond = jnp.concatenate([values[:, dilation:, :], padding], axis=1)
    return before, beyond


def cell_inner(incoming, tap_rows, dilation):
    values = incoming.astype(jnp.float32)
    before, beyond = shifted(values, dilation)
    hidden = tap_rows[0] * before + tap_rows[1] * values + tap_rows[2] * beyond
    activated = (hidden * jax.nn.sigmoid(hidden)).astype(jnp.bfloat16)
    return values, before, beyond, hidden, activated


def cell_forward(incoming, tap_rows, matrix, dilation):
    values, before, beyond, hidden, activated = cell_inner(incoming, tap_rows, dilation)
    channels = matrix.shape[0]
    branch = jnp.dot(activated.reshape(-1, channels), matrix, preferred_element_type=jnp.float32)
    return (values + branch.reshape(values.shape)).astype(jnp.bfloat16)


def cell_backward(incoming, tap_rows, matrix, dilation, upstream):
    values, before, beyond, hidden, activated = cell_inner(incoming, tap_rows, dilation)
    channels = matrix.shape[0]
    flat_grad = upstream.astype(jnp.bfloat16).reshape(-1, channels)
    grad_matrix = lax.dot_general(activated.reshape(-1, channels), flat_grad, (((0,), (0,)), ((), ())), preferred_element_type=jnp.float32)
    grad_active = lax.dot_general(flat_grad, matrix, (((1,), (1,)), ((), ())), preferred_element_type=jnp.float32).reshape(values.shape)
    sigmoid_part = jax.nn.sigmoid(hidden)
    grad_hidden = grad_active * sigmoid_part * (1.0 + hidden * (1.0 - sigmoid_part))
    grad_tap = jnp.stack([jnp.sum(grad_hidden * before, axis=(0, 1)), jnp.sum(grad_hidden * values, axis=(0, 1)), jnp.sum(grad_hidden * beyond, axis=(0, 1))])
    spread_before, spread_beyond = shifted(grad_hidden, dilation)
    grad_in = upstream + tap_rows[0] * spread_beyond + tap_rows[1] * grad_hidden + tap_rows[2] * spread_before
    return grad_in, grad_matrix, grad_tap


def reference(images, cotangent, section_cells, point_weight, tap_weight):
    cell_count = point_weight.shape[0]
    channels = point_weight.shape[1]
    positions = jnp.arange(cell_count).astype(jnp.int32)
    section_of = positions // CELLS_DEV
    live_cells = (positions % CELLS_DEV) < section_cells[section_of]
    pair_live = live_cells.reshape(cell_count // 2, 2)
    pair_matrix = point_weight.reshape(cell_count // 2, 2, channels, channels)
    pair_taps = tap_weight.reshape(cell_count // 2, 2, 3, channels)
    total_point = jnp.zeros((cell_count, channels, channels), jnp.float32)
    total_taps = jnp.zeros((cell_count, 3, channels), jnp.float32)

    def forward_pair(running, pieces):
        matrices, taps_pair, active_flags = pieces
        stored = []
        for within in range(2):
            stored.append(running)
            produced = cell_forward(running, taps_pair[within], matrices[within], 1 + within)
            running = jnp.where(active_flags[within], produced, running)
        return running, jnp.stack(stored)

    def backward_pair(upstream, pieces):
        matrices, taps_pair, active_flags, inputs_pair = pieces
        point_parts = [None, None]
        tap_parts = [None, None]
        for within in (1, 0):
            grad_in, grad_matrix, grad_tap = cell_backward(inputs_pair[within], taps_pair[within], matrices[within], 1 + within, upstream)
            upstream = jnp.where(active_flags[within], grad_in, upstream)
            point_parts[within] = jnp.where(active_flags[within], grad_matrix, 0.0)
            tap_parts[within] = jnp.where(active_flags[within], grad_tap, 0.0)
        return upstream, (jnp.stack(point_parts), jnp.stack(tap_parts))

    for micro_index in range(MICRO):
        last_output, kept_inputs = lax.scan(forward_pair, images[micro_index], (pair_matrix, pair_taps, pair_live))
        first_grad, grads_pair = lax.scan(backward_pair, cotangent[micro_index].astype(jnp.float32), (pair_matrix, pair_taps, pair_live, kept_inputs), reverse=True)
        total_point = total_point + grads_pair[0].reshape(cell_count, channels, channels)
        total_taps = total_taps + grads_pair[1].reshape(cell_count, 3, channels)
    return total_point, total_taps
```

```python
import functools

import jax
import jax.numpy as jnp
from jax import lax
from jax.experimental import pallas as pl
from jax.experimental.pallas import tpu as pltpu
from jax.sharding import PartitionSpec as P


F32, BF16 = jnp.float32, jnp.bfloat16
SUB, LANES = 8, 128
VMEM_LIMIT = 16 << 20


def rotated(tiles, up):
    moved = pltpu.roll(tiles, SUB - 1 if up else 1, axis=2)
    place = lax.broadcasted_iota(jnp.int32, tiles.shape, 2)
    return jnp.where(place == (SUB - 1 if up else 0), 0.0, moved)


def shifted(v, d):
    count = v.shape[1]
    before = jnp.concatenate([rotated(v[:, count - d :], False), v[:, : count - d]], axis=1)
    beyond = jnp.concatenate([v[:, d:], rotated(v[:, :d], True)], axis=1)
    return before, beyond


def tile_view(flat, width):
    return flat.reshape(-1, width // SUB, SUB, flat.shape[-1])


def load_tiled(x_ref, stage_ref, v_ref, width, tiled):
    if tiled:
        v_ref[...] = x_ref[...].astype(F32)
        return
    count = width // SUB
    for lane in range(stage_ref.shape[0]):
        columns = slice(lane * LANES, (lane + 1) * LANES)
        stage_ref[lane] = x_ref[:, columns].astype(F32)
        for image in range(x_ref.shape[0] // width):
            for j in range(count):
                tile = stage_ref[lane, pl.ds(image * width + j, SUB, stride=count), :]
                v_ref[image * width + j * SUB : image * width + (j + 1) * SUB, columns] = tile


def forward_kernel(width, stage, chunk, n_ref, x_ref, w_ref, t_ref, *refs):
    y_ref, sx, sa, sd, v_ref, stage_ref = refs[-6:]
    x_ref = x_ref.at[chunk] if stage == 0 else x_ref
    rows, channels = x_ref.shape
    row0 = chunk * rows
    live = n_ref[stage]

    def cell(k, d):
        flat = v_ref[...]
        v = tile_view(flat, width)
        sx[k, pl.ds(row0, rows), :] = flat.astype(BF16)
        before, beyond = shifted(v, d)
        taps = t_ref[k]
        h = taps[0:1] * before + taps[1:2] * v + taps[2:3] * beyond
        s = 0.5 * jnp.tanh(0.5 * h) + 0.5
        a = h * s
        sd[k, pl.ds(row0, rows), :] = (s + a * (1.0 - s)).reshape(rows, channels)
        act = a.reshape(rows, channels).astype(BF16)
        sa[k, pl.ds(row0, rows), :] = act
        branch = jnp.dot(act, w_ref[k], preferred_element_type=F32)
        v_ref[...] = (flat + branch).astype(BF16).astype(F32)

    @pl.when(live > 0)
    def _():
        load_tiled(x_ref, stage_ref, v_ref, width, stage > 0)

        @pl.loop(0, (live + 1) // 2)
        def _(pair):
            cell(2 * pair, 1)

            @pl.when(2 * pair + 1 < live)
            def _():
                cell(2 * pair + 1, 2)

        y_ref[...] = v_ref[...].astype(BF16)


def backward_kernel(width, stage, chunk, entry, n_ref, x_ref, w_ref, t_ref, sx, sd, *refs):
    y_ref, sg, st, v_ref, stage_ref = refs[-5:]
    x_ref = x_ref.at[chunk] if entry else x_ref
    rows, channels = x_ref.shape
    row0 = chunk * rows
    live = n_ref[stage]

    def cell(k, d):
        up = v_ref[...]
        gr = up.astype(BF16)
        sg[k, pl.ds(row0, rows), :] = gr
        ga = lax.dot_general(gr, w_ref[k], (((1,), (1,)), ((), ())), preferred_element_type=F32)
        gh = tile_view(ga * sd[k, pl.ds(row0, rows), :], width)
        values = tile_view(sx[k, pl.ds(row0, rows), :].astype(F32), width)
        before, beyond = shifted(values, d)
        for i, other in enumerate((before, values, beyond)):
            st[k, i] += jnp.sum(gh * other, axis=(0, 1))
        taps = t_ref[k]
        g_before, g_beyond = shifted(gh, d)
        step = taps[0:1] * g_beyond + taps[1:2] * gh + taps[2:3] * g_before
        v_ref[...] = up + step.reshape(rows, channels)

    @pl.when(live > 0)
    def _():
        load_tiled(x_ref, stage_ref, v_ref, width, not entry)
        if row0 == 0:
            st[...] = jnp.zeros_like(st)

        pairs = (live + 1) // 2

        @pl.loop(0, pairs)
        def _(step):
            pair = pairs - 1 - step

            @pl.when(2 * pair + 1 < live)
            def _():
                cell(2 * pair + 1, 2)

            cell(2 * pair, 1)

        y_ref[...] = v_ref[...].astype(BF16)


def weight_kernel(blocks, s_ref, sa, sg, st, keep_ref, send_ref):
    live, me = s_ref[s_ref.shape[0] - 2], s_ref[s_ref.shape[0] - 1]
    slots, _, channels = sa.shape
    share = channels // blocks

    @pl.loop(0, slots)
    def _(k):
        def put(grad):
            for j in range(blocks):
                place = jnp.bitwise_xor(j, me)
                piece = grad[j * share : (j + 1) * share]

                @pl.when(jnp.bitwise_and(place, 1) == 0)
                def _():
                    keep_ref[place // 2, pl.ds(pl.multiple_of(k * share, share), share), :] = piece

                @pl.when(jnp.bitwise_and(place, 1) == 1)
                def _():
                    send_ref[place // 2, pl.ds(pl.multiple_of(k * share, share), share), :] = piece

        @pl.when(k < live)
        def _():
            grad = lax.dot_general(sa[k], sg[k], (((0,), (0,)), ((), ())), preferred_element_type=F32)
            put(grad.astype(BF16))

        @pl.when(k >= live)
        def _():
            put(jnp.zeros((channels, channels), BF16))


def whole(n):
    return [pl.BlockSpec(memory_space=pltpu.VMEM)] * n


SMEM = pl.BlockSpec(memory_space=pltpu.SMEM)


def params():
    return pltpu.CompilerParams(vmem_limit_bytes=VMEM_LIMIT, has_side_effects=False)


def per_device(images, cotangent, section_cells, point_weight, tap_weight):
    micro, images_dev, width, channels = images.shape
    slots = point_weight.shape[0]
    segments = lax.axis_size("segment")
    blocks = lax.axis_size("dp")
    place, me = lax.axis_index("segment"), lax.axis_index("dp")
    rows = images_dev * width
    total = micro * rows
    here = jnp.arange(segments) == place
    counts = jnp.where(here, section_cells, 0).astype(jnp.int32)
    live = jnp.sum(counts)
    plan = jnp.concatenate([counts, jnp.stack([live, me.astype(jnp.int32)])])
    xs = images.reshape(micro, rows, channels)
    cs = cotangent.reshape(micro, rows, channels)

    def vm(shape, dtype):
        return pltpu.VMEM(shape, dtype)

    scratch = [pltpu.VMEM((rows, channels), F32), pltpu.VMEM((channels // LANES, rows, LANES), F32)]

    def near(*arrays):
        return [pltpu.with_memory_space_constraint(a, pltpu.VMEM) for a in arrays]

    arriving = [xs] * micro
    kept = [vm((slots, total, channels), t) for t in (BF16, BF16, F32)]
    saved = []
    for stage in range(segments):
        leaving = []
        for m in range(micro):
            y, *saved = pl.pallas_call(
                functools.partial(forward_kernel, width, stage, m),
                out_shape=[vm((rows, channels), BF16)] + kept,
                in_specs=[SMEM] + whole(3 + len(saved)),
                out_specs=whole(4),
                input_output_aliases={4 + i: 1 + i for i in range(len(saved))},
                scratch_shapes=scratch,
                compiler_params=params(),
                name="forward",
            )(plan, *near(arriving[m], point_weight, tap_weight, *saved))
            if stage + 1 < segments:
                leaving.append(lax.ppermute(y, "segment", [(stage, stage + 1)]))
        arriving = leaving
    sx, sa, sd = saved

    arriving = [cs] * micro
    kept = [vm((slots, total, channels), BF16), vm((slots, 3, SUB, channels), F32)]
    saved = []
    for stage in reversed(range(segments)):
        leaving = []
        for m in range(micro):
            y, *saved = pl.pallas_call(
                functools.partial(backward_kernel, width, stage, m, stage + 1 == segments),
                out_shape=[vm((rows, channels), BF16)] + kept,
                in_specs=[SMEM] + whole(5 + len(saved)),
                out_specs=whole(3),
                input_output_aliases={6 + i: 1 + i for i in range(len(saved))},
                scratch_shapes=scratch,
                compiler_params=params(),
                name="backward",
            )(plan, *near(arriving[m], point_weight, tap_weight, sx, sd, *saved))
            if stage > 0:
                leaving.append(lax.ppermute(y, "segment", [(stage, stage - 1)]))
        arriving = leaving
    sg, st = saved

    share = channels // blocks
    half = blocks // 2
    keep, send = pl.pallas_call(
        functools.partial(weight_kernel, blocks),
        out_shape=[jax.ShapeDtypeStruct((half, slots * share, channels), BF16)] * 2,
        in_specs=[SMEM] + whole(3),
        out_specs=whole(2),
        compiler_params=params(),
        name="weights",
    )(plan, *near(sa, sg, st))
    slot_live = (jnp.arange(slots) < live)[:, None, None]
    taps = jnp.where(slot_live, jnp.sum(st, axis=2), 0.0).reshape(slots * 3, channels)

    def swap(value, mask):
        return lax.ppermute(value, "dp", [(i, i ^ mask) for i in range(blocks)])

    def halves(t):
        high = t.astype(BF16)
        return jnp.concatenate([high, (t - high.astype(F32)).astype(BF16)], axis=0)

    def joined(p):
        return p[: slots * 3].astype(F32) + p[slots * 3 :].astype(F32)

    got = swap(send, 1)
    got_taps = swap(halves(taps), 1)
    mine = keep.astype(F32) + got.astype(F32)
    taps = taps + joined(got_taps)
    step = 2
    while step < blocks:
        wide = 4 if step * 4 <= blocks else 2
        parts = mine.reshape(-1, wide, slots * share, channels)
        tap_rows = halves(taps)
        mine = parts[:, 0]
        flat = mine.shape[0] * slots * share
        for other in range(1, wide):
            payload = jnp.concatenate([parts[:, other].reshape(flat, channels).astype(BF16), tap_rows], axis=0)
            got = swap(payload, other * step)
            mine = mine + got[:flat].reshape(mine.shape).astype(F32)
            taps = taps + joined(got[flat:])
        step *= wide
    return mine.reshape(slots, share, channels), taps.reshape(slots, 3, channels)


def solution(mesh):
    placed = (
        P(None, "dp", None, None),
        P(None, "dp", None, None),
        P(),
        P("segment", None, None),
        P("segment", None, None),
    )
    return jax.shard_map(
        per_device,
        mesh=mesh,
        in_specs=placed,
        out_specs=(P("segment", "dp", None), P("segment", None, None)),
        check_vma=False,
    )
```

```python
import functools

import jax
import jax.numpy as jnp
from jax import lax
from jax.experimental import pallas as pl
from jax.experimental.pallas import tpu as pltpu
from jax.sharding import PartitionSpec as P


F32, BF16 = jnp.float32, jnp.bfloat16
SUB, LANES = 8, 128
VMEM_LIMIT = 16 << 20
TAPS = 3
GROUP = 2


def rotated(tiles, up):
    moved = pltpu.roll(tiles, SUB - 1 if up else 1, axis=2)
    place = lax.broadcasted_iota(jnp.int32, tiles.shape, 2)
    return jnp.where(place == (SUB - 1 if up else 0), 0.0, moved)


def shifted(v, d):
    count = v.shape[1]
    before = jnp.concatenate([rotated(v[:, count - d :], False), v[:, : count - d]], axis=1)
    beyond = jnp.concatenate([v[:, d:], rotated(v[:, :d], True)], axis=1)
    return before, beyond


def tile_view(flat, width):
    return flat.reshape(-1, width // SUB, SUB, flat.shape[-1])


def load_plain(x_ref, stage_ref, v_ref, width):
    count = width // SUB
    for lane in range(stage_ref.shape[0]):
        columns = slice(lane * LANES, (lane + 1) * LANES)
        stage_ref[lane] = x_ref[:, columns].astype(F32)
        for image in range(x_ref.shape[0] // width):
            for j in range(count):
                tile = stage_ref[lane, pl.ds(image * width + j, SUB, stride=count), :]
                v_ref[image * width + j * SUB : image * width + (j + 1) * SUB, columns] = tile


def taps_of(t_ref, k):
    return [t_ref[i, pl.ds(k, 1), :] for i in range(TAPS)]


def run_forward(width, row0, live, w_ref, t_ref, sx, sa, sd, v_ref):
    rows, channels = v_ref.shape

    def cell(k, d):
        flat = v_ref[...]
        v = tile_view(flat, width)
        sx[k, pl.ds(row0, rows), :] = flat.astype(BF16)
        before, beyond = shifted(v, d)
        t0, t1, t2 = taps_of(t_ref, k)
        h = t0 * before + t1 * v + t2 * beyond
        s = 0.5 * jnp.tanh(0.5 * h) + 0.5
        a = h * s
        sd[k, pl.ds(row0, rows), :] = (s + a * (1.0 - s)).reshape(rows, channels)
        act = a.reshape(rows, channels).astype(BF16)
        sa[k, pl.ds(row0, rows), :] = act
        branch = jnp.dot(act, w_ref[k], preferred_element_type=F32)
        v_ref[...] = (flat + branch).astype(BF16).astype(F32)

    @pl.loop(0, (live + 1) // 2)
    def _(pair):
        cell(2 * pair, 1)

        @pl.when(2 * pair + 1 < live)
        def _():
            cell(2 * pair + 1, 2)


def run_backward(width, row0, live, w_ref, t_ref, sd, sg, sh, v_ref):
    rows, channels = v_ref.shape

    def cell(k, d):
        up = v_ref[...]
        gr = up.astype(BF16)
        sg[k, pl.ds(row0, rows), :] = gr
        ga = lax.dot_general(gr, w_ref[k], (((1,), (1,)), ((), ())), preferred_element_type=F32)
        gh = ga * sd[k, pl.ds(row0, rows), :]
        sh[k, pl.ds(row0, rows), :] = gh
        gh = tile_view(gh, width)
        t0, t1, t2 = taps_of(t_ref, k)
        before, beyond = shifted(gh, d)
        step = t0 * beyond + t1 * gh + t2 * before
        v_ref[...] = up + step.reshape(rows, channels)

    pairs = (live + 1) // 2

    @pl.loop(0, pairs)
    def _(step):
        pair = pairs - 1 - step

        @pl.when(2 * pair + 1 < live)
        def _():
            cell(2 * pair + 1, 2)

        cell(2 * pair, 1)


def setup_kernel(cells_in, images_in, cotangent_in, weights_in, taps_in, cells, images, cotangent, weights, taps, sems):
    pairs = ((cells_in, cells), (images_in, images), (weights_in, weights), (taps_in, taps), (cotangent_in, cotangent))
    copies = [pltpu.make_async_copy(a, b, sems.at[i]) for i, (a, b) in enumerate(pairs)]
    for copy in copies:
        copy.start()
    for copy in copies:
        copy.wait()


def forward_kernel(width, stage, chunk, n_ref, x_ref, w_ref, t_ref, *refs):
    y_ref, sx, sa, sd, v_ref, stage_ref = refs[-6:]

    @pl.when(lax.axis_index("segment") == stage)
    def _():
        if stage == 0:
            load_plain(x_ref.at[chunk], stage_ref, v_ref, width)
        else:
            v_ref[...] = x_ref[...].astype(F32)
        run_forward(width, chunk * v_ref.shape[0], n_ref[stage], w_ref, t_ref, sx, sa, sd, v_ref)
        y_ref[...] = v_ref[...].astype(BF16)


def turn_kernel(width, stage, chunk, n_ref, x_ref, c_ref, w_ref, t_ref, *refs):
    y_ref, sx, sa, sd, sg, sh, v_ref, stage_ref = refs[-8:]

    @pl.when(lax.axis_index("segment") == stage)
    def _():
        row0, live = chunk * v_ref.shape[0], n_ref[stage]
        if stage == 0:
            load_plain(x_ref.at[chunk], stage_ref, v_ref, width)
        else:
            v_ref[...] = x_ref[...].astype(F32)
        run_forward(width, row0, live, w_ref, t_ref, sx, sa, sd, v_ref)
        load_plain(c_ref.at[chunk], stage_ref, v_ref, width)
        run_backward(width, row0, live, w_ref, t_ref, sd, sg, sh, v_ref)
        y_ref[...] = v_ref[...].astype(BF16)


def backward_kernel(width, stage, chunk, n_ref, x_ref, w_ref, t_ref, sd, *refs):
    sg, sh, v_ref = refs[-3:]

    @pl.when(lax.axis_index("segment") == stage)
    def _():
        v_ref[...] = x_ref[...].astype(F32)
        run_backward(width, chunk * v_ref.shape[0], n_ref[stage], w_ref, t_ref, sd, sg, sh, v_ref)
        if stage > 0:
            refs[-4][...] = v_ref[...].astype(BF16)


def halves(t):
    high = t.astype(BF16)
    return high, (t - high.astype(F32)).astype(BF16)


def weight_kernel(width, rows, chunk, last, blocks, n_ref, sx, sa, sg0, sh0, *refs):
    if last:
        sg, sh, keep_ref, taps_ref, send_ref, tap_scr = refs[-6:]
        total, tapsum = refs[:2]
    else:
        sg, sh, total, tapsum = refs[-4:]
    live = n_ref[lax.axis_index("segment")]
    slots, _, channels = sa.shape
    share = channels // blocks
    span = slice(chunk * rows, (chunk + 1) * rows)

    def grads(k, d):
        grad = lax.dot_general(sa[k, span], sg[k, span], (((0,), (0,)), ((), ())), preferred_element_type=F32)
        values = tile_view(sx[k, span].astype(F32), width)
        gh = tile_view(sh[k, span], width)
        before, beyond = shifted(values, d)
        sums = [jnp.sum(gh * other, axis=(0, 1)) for other in (before, values, beyond)]
        return grad, sums

    if not last:

        def one(k, d):
            @pl.when(k < live)
            def _():
                grad, sums = grads(k, d)
                if chunk == 0:
                    total[k] = grad
                    for i in range(TAPS):
                        tapsum[k, i] = sums[i]
                else:
                    total[k] += grad
                    for i in range(TAPS):
                        tapsum[k, i] += sums[i]

        @pl.loop(0, slots // 2)
        def _(pair):
            one(2 * pair, 1)
            one(2 * pair + 1, 2)

        return

    me = lax.axis_index("dp")

    def put(k, grad):
        for j in range(blocks):
            place = jnp.bitwise_xor(j, me)
            piece = grad[j * share : (j + 1) * share]
            spot = pl.ds(pl.multiple_of(k * share, share), share)

            @pl.when(jnp.bitwise_and(place, 1) == 0)
            def _():
                keep_ref[place // 2, spot, :] = piece

            @pl.when(jnp.bitwise_and(place, 1) == 1)
            def _():
                send_ref[pl.ds(pl.multiple_of(place // 2 * (slots * share) + k * share, share), share), :] = piece.astype(BF16)

    def one(k, d):
        @pl.when(k < live)
        def _():
            grad, sums = grads(k, d)
            if chunk > 0:
                grad = grad + total[k]
                sums = [sums[i] + tapsum[k, i] for i in range(TAPS)]
            put(k, grad)
            for i in range(TAPS):
                tap_scr[i, pl.ds(k, 1), :] = jnp.sum(sums[i], axis=0, keepdims=True)

        @pl.when(k >= live)
        def _():
            put(k, jnp.zeros((channels, channels), F32))
            for i in range(TAPS):
                tap_scr[i, pl.ds(k, 1), :] = jnp.zeros((1, channels), F32)

    @pl.loop(0, slots // 2)
    def _(pair):
        one(2 * pair, 1)
        one(2 * pair + 1, 2)

    taps = tap_scr[...].reshape(TAPS * slots, channels)
    taps_ref[...] = taps
    high, low = halves(taps)
    base = send_ref.shape[0] - 2 * TAPS * slots
    send_ref[base : base + TAPS * slots, :] = high
    send_ref[base + TAPS * slots :, :] = low


def merge_kernel(wide, own_ref, taps_ref, *refs):
    incoming = refs[: len(refs) - (wide + 1)]
    outs = refs[len(refs) - (wide + 1) :]
    tap_rows = taps_ref.shape[0]
    groups, block, channels = own_ref.shape
    rest = groups // wide
    flat = groups * block
    taps = taps_ref[...]
    for ref in incoming:
        taps = taps + (ref[flat : flat + tap_rows].astype(F32) + ref[flat + tap_rows :].astype(F32))
    high, low = halves(taps)
    for g in range(groups):
        value = own_ref[g]
        for ref in incoming:
            value = value + ref[g * block : (g + 1) * block].astype(F32)
        to, at = g % wide, g // wide
        if to == 0:
            outs[0][at] = value
        else:
            outs[1 + to][at * block : (at + 1) * block] = value.astype(BF16)
    outs[1][...] = taps
    for ref in outs[2:]:
        ref[rest * block : rest * block + tap_rows] = high
        ref[rest * block + tap_rows :] = low


def whole(n):
    return [pl.BlockSpec(memory_space=pltpu.VMEM)] * n


SMEM = pl.BlockSpec(memory_space=pltpu.SMEM)


def params():
    return pltpu.CompilerParams(vmem_limit_bytes=VMEM_LIMIT)


def near(*arrays):
    return [pltpu.with_memory_space_constraint(a, pltpu.VMEM) for a in arrays]


def per_device(images, cotangent, section_cells, point_weight, tap_weight):
    micro, images_dev, width, channels = images.shape
    slots = point_weight.shape[0]
    segments = lax.axis_size("segment")
    blocks = lax.axis_size("dp")
    micro, images_dev = micro // GROUP, images_dev * GROUP
    rows = images_dev * width
    total = micro * rows
    vm = pltpu.VMEM

    def vmlike(a):
        return vm(a.shape, a.dtype)

    raw = [
        section_cells,
        images.reshape(micro, rows, channels),
        cotangent.reshape(micro, rows, channels),
        point_weight,
        tap_weight.transpose(1, 0, 2),
    ]
    cells, xs, cs, weights, taps = pl.pallas_call(
        setup_kernel,
        out_shape=[pltpu.SMEM(section_cells.shape, section_cells.dtype)] + [vmlike(a) for a in raw[1:]],
        in_specs=[pl.BlockSpec(memory_space=pltpu.HBM)] * 5,
        out_specs=[SMEM] + whole(4),
        scratch_shapes=[pltpu.SemaphoreType.DMA((5,))],
        compiler_params=params(),
        name="setup",
    )(*[pltpu.with_memory_space_constraint(a, pltpu.HBM) for a in raw])
    cells = pltpu.with_memory_space_constraint(cells, pltpu.SMEM)

    wide_scratch = [vm((rows, channels), F32), vm((channels // LANES, rows, LANES), F32)]
    out_y = vm((rows, channels), BF16)
    kept = [vm((slots, total, channels), t) for t in (BF16, BF16, F32)]
    kept_back = [vm((slots, total, channels), t) for t in (BF16, F32)]

    def stage_call(kernel, name, inputs, state, state_shapes, scratch, leaves=True):
        front = [out_y] * leaves
        return pl.pallas_call(
            kernel,
            out_shape=front + state_shapes,
            in_specs=[SMEM] + whole(len(inputs) + len(state)),
            out_specs=whole(len(front) + len(state_shapes)),
            input_output_aliases={1 + len(inputs) + i: len(front) + i for i in range(len(state))},
            scratch_shapes=scratch,
            compiler_params=params(),
            name=name,
        )(cells, *near(*inputs, *state))

    arriving = [xs] * micro
    saved = []
    for stage in range(segments - 1):
        leaving = []
        for m in range(micro):
            y, *saved = stage_call(
                functools.partial(forward_kernel, width, stage, m),
                "forward",
                [arriving[m], weights, taps],
                saved,
                kept,
                wide_scratch,
            )
            leaving.append(lax.ppermute(y, "segment", [(stage, stage + 1)]))
        arriving = leaving

    back = []
    leaving = []
    for m in range(micro):
        y, *state = stage_call(
            functools.partial(turn_kernel, width, segments - 1, m),
            "turn",
            [arriving[m], cs, weights, taps],
            [*saved, *back],
            kept + kept_back,
            wide_scratch,
        )
        saved, back = state[:3], state[3:]
        if segments > 1:
            leaving.append(lax.ppermute(y, "segment", [(segments - 1, segments - 2)]))
        saved = list(saved)
    arriving = leaving
    sx, sa, sd = saved

    share = channels // blocks
    half = blocks // 2
    block = slots * share
    extra = 2 * TAPS * slots
    sums = []

    def weight_call(m, back, sums):
        last = m == micro - 1
        if last:
            out_shape = [vmlike(a) for a in back] + [
                vm((half, block, channels), F32),
                vm((TAPS * slots, channels), F32),
                vm((half * block + extra, channels), BF16),
            ]
            scratch = [vm((TAPS, slots, channels), F32)]
        else:
            out_shape = [vmlike(a) for a in back] + [
                vm((slots, channels, channels), F32),
                vm((slots, TAPS, SUB, channels), F32),
            ]
            scratch = []
        aliases = {3: 0, 4: 1}
        if sums and not last:
            aliases |= {5: 2, 6: 3}
        return pl.pallas_call(
            functools.partial(weight_kernel, width, rows, m, last, blocks),
            out_shape=out_shape,
            in_specs=[SMEM] + whole(4 + len(sums)),
            out_specs=whole(len(out_shape)),
            input_output_aliases=aliases,
            scratch_shapes=scratch,
            compiler_params=params(),
            name="weights",
        )(cells, *near(sx, sa, *back, *sums))

    for stage in reversed(range(segments - 1)):
        leaving = []
        for m in range(micro):
            *y, a, b = stage_call(
                functools.partial(backward_kernel, width, stage, m),
                "backward",
                [arriving[m], weights, taps, sd],
                back,
                kept_back,
                wide_scratch[:1],
                stage > 0,
            )
            back = [a, b]
            if stage > 0:
                leaving.append(lax.ppermute(y[0], "segment", [(stage, stage - 1)]))
            else:
                out = weight_call(m, back, sums)
                back, sums = out[:2], out[2:]
        arriving = leaving
    if segments == 1:
        for m in range(micro):
            out = weight_call(m, back, sums)
            back, sums = out[:2], out[2:]
    own, tap_total, send = sums

    def swap(value, mask):
        return lax.ppermute(value, "dp", [(i, i ^ mask) for i in range(blocks)])

    incoming = [swap(send, 1)] if blocks > 1 else []
    step = 2
    while True:
        groups = blocks // step
        wide = min(4, groups)
        final = groups == 1
        out_shape = [vm((groups // wide, block, channels), F32), vm((TAPS * slots, channels), F32)]
        out_shape += [vm((groups // wide * block + extra, channels), BF16)] * (wide - 1)
        if final:
            out_shape = [jax.ShapeDtypeStruct(a.shape, a.dtype) for a in out_shape]
        own, tap_total, *sends = pl.pallas_call(
            functools.partial(merge_kernel, wide),
            out_shape=out_shape,
            in_specs=whole(2 + len(incoming)),
            out_specs=whole(len(out_shape)),
            compiler_params=params(),
            name="merge",
        )(*near(own, tap_total, *incoming))
        if final:
            break
        incoming = [swap(value, (i + 1) * step) for i, value in enumerate(sends)]
        step *= wide
    return own.reshape(slots, share, channels), tap_total.reshape(TAPS, slots, channels).transpose(1, 0, 2)


def solution(mesh):
    placed = (
        P(None, "dp", None, None),
        P(None, "dp", None, None),
        P(),
        P("segment", None, None),
        P("segment", None, None),
    )
    return jax.shard_map(
        per_device,
        mesh=mesh,
        in_specs=placed,
        out_specs=(P("segment", "dp", None), P("segment", None, None)),
        check_vma=False,
    )
```
